32 devices in a mesh: dp: 16 (over z, y, core), seq: 2 (over x).
Axes of the slice: x: 2, y: 2, z: 4, core: 2. Of those that a mesh axis runs over, the one named last changes fastest.
Arguments:
- latents: float32 [16, 256, 1152], P('dp', 'seq'), may hold values from -6 to 6
- condition: float32 [8, 1152], replicated, may hold values from -6 to 6
- slot_latent: int32 [16, 1], P('dp'), may hold values from 0 to 7, as said below
- slot_counts: int32 [16], P('dp'), may hold values from 0 to 1, as said below
- output_gradient: float32 [16, 256, 1152], P('dp', 'seq'), may hold values from -6 to 6
- ada_weight: float32 [1152, 6912], P(None, ('dp', 'seq')), may hold values from -0.1875 to 0.1875
- ada_bias: float32 [6912], P(('dp', 'seq')), may hold values from -1.75 to 1.75
- qkv_weight: float32 [1152, 3456], P('dp', 'seq'), may hold values from -5 to 5, as said below
- qkv_bias: float32 [3456], P('seq'), may hold values from -1.25 to 1.25
- out_weight: float32 [1152, 1152], P('dp', 'seq'), may hold values from -0.75 to 0.75
- out_bias: float32 [1152], P('seq'), may hold values from -1.25 to 1.25
- up_weight: float32 [1152, 4608], P('dp', 'seq'), may hold values from -0.1875 to 0.1875
- up_bias: float32 [4608], P('seq'), may hold values from -1.25 to 1.25
- down_weight: float32 [4608, 1152], P('dp', 'seq'), may hold values from -0.09375 to 0.09375
- down_bias: float32 [1152], P('seq'), may hold values from -1.25 to 1.25
- mean_adaw: float32 [1152, 6912], P(None, ('dp', 'seq')), may hold values from -16 to 16
- mean_adab: float32 [6912], P(('dp', 'seq')), may hold values from -16 to 16
- mean_qkvw: float32 [1152, 3456], P('dp', 'seq'), may hold values from -16 to 16
- mean_qkvb: float32 [3456], P('seq'), may hold values from -16 to 16
- mean_outw: float32 [1152, 1152], P('dp', 'seq'), may hold values from -16 to 16
- mean_outb: float32 [1152], P('seq'), may hold values from -16 to 16
- mean_upw: float32 [1152, 4608], P('dp', 'seq'), may hold values from -16 to 16
- mean_upb: float32 [4608], P('seq'), may hold values from -16 to 16
- mean_downw: float32 [4608, 1152], P('dp', 'seq'), may hold values from -16 to 16
- mean_downb: float32 [1152], P('seq'), may hold values from -16 to 16
- sqmean_adaw: float32 [1152, 6912], P(None, ('dp', 'seq')), may hold values from 0.3 to 3
- sqmean_adab: float32 [6912], P(('dp', 'seq')), may hold values from 0.3 to 3
- sqmean_qkvw: float32 [1152, 3456], P('dp', 'seq'), may hold values from 0.3 to 3
- sqmean_qkvb: float32 [3456], P('seq'), may hold values from 0.3 to 3
- sqmean_outw: float32 [1152, 1152], P('dp', 'seq'), may hold values from 0.3 to 3
- sqmean_outb: float32 [1152], P('seq'), may hold values from 0.3 to 3
- sqmean_upw: float32 [1152, 4608], P('dp', 'seq'), may hold values from 0.3 to 3
- sqmean_upb: float32 [4608], P('seq'), may hold values from 0.3 to 3
- sqmean_downw: float32 [4608, 1152], P('dp', 'seq'), may hold values from 0.3 to 3
- sqmean_downb: float32 [1152], P('seq'), may hold values from 0.3 to 3
Outputs:
- block_output: float32 [16, 256, 1152], P('dp', 'seq')
- latent_gradient: float32 [16, 256, 1152], P('dp', 'seq')
- condition_grad: float32 [8, 1152], replicated
- grad_adaw: float32 [1152, 6912], P(None, ('dp', 'seq'))
- grad_adab: float32 [6912], P(('dp', 'seq'))
- grad_qkvw: float32 [1152, 3456], P('dp', 'seq')
- grad_qkvb: float32 [3456], P('seq')
- grad_outw: float32 [1152, 1152], P('dp', 'seq')
- grad_outb: float32 [1152], P('seq')
- grad_upw: float32 [1152, 4608], P('dp', 'seq')
- grad_upb: float32 [4608], P('seq')
- grad_downw: float32 [4608, 1152], P('dp', 'seq')
- grad_downb: float32 [1152], P('seq')
- newval_adaw: float32 [1152, 6912], P(None, ('dp', 'seq'))
- newval_adab: float32 [6912], P(('dp', 'seq'))
- newval_qkvw: float32 [1152, 3456], P('dp', 'seq')
- newval_qkvb: float32 [3456], P('seq')
- newval_outw: float32 [1152, 1152], P('dp', 'seq')
- newval_outb: float32 [1152], P('seq')
- newval_upw: float32 [1152, 4608], P('dp', 'seq')
- newval_upb: float32 [4608], P('seq')
- newval_downw: float32 [4608, 1152], P('dp', 'seq')
- newval_downb: float32 [1152], P('seq')
- newmean_adaw: float32 [1152, 6912], P(None, ('dp', 'seq'))
- newmean_adab: float32 [6912], P(('dp', 'seq'))
- newmean_qkvw: float32 [1152, 3456], P('dp', 'seq')
- newmean_qkvb: float32 [3456], P('seq')
- newmean_outw: float32 [1152, 1152], P('dp', 'seq')
- newmean_outb: float32 [1152], P('seq')
- newmean_upw: float32 [1152, 4608], P('dp', 'seq')
- newmean_upb: float32 [4608], P('seq')
- newmean_downw: float32 [4608, 1152], P('dp', 'seq')
- newmean_downb: float32 [1152], P('seq')
- newsqr_adaw: float32 [1152, 6912], P(None, ('dp', 'seq'))
- newsqr_adab: float32 [6912], P(('dp', 'seq'))
- newsqr_qkvw: float32 [1152, 3456], P('dp', 'seq')
- newsqr_qkvb: float32 [3456], P('seq')
- newsqr_outw: float32 [1152, 1152], P('dp', 'seq')
- newsqr_outb: float32 [1152], P('seq')
- newsqr_upw: float32 [1152, 4608], P('dp', 'seq')
- newsqr_upb: float32 [4608], P('seq')
- newsqr_downw: float32 [4608, 1152], P('dp', 'seq')
- newsqr_downb: float32 [1152], P('seq')
The draws below stay inside these ranges and needn't reach their ends.
Inputs may be any that keep to these rules, and one draw needn't show every extreme that they name: `slot_counts`: live slots of a group come first; the entries sum to 8; some group has all 1 slots live in every draw, some groups may have none. `slot_latent`: the live slots name every latent exactly once; entries of slots that are not live are arbitrary latents. `qkv_weight`: query and value columns have entries of order 1152^-1/2; key columns may have entries up to the ends of the range.
All inputs are finite; a program needn't handle non-finite values.
Results may differ from the reference program's by a relative error of at most 0.012.
The reference program's roundings to bfloat16 on the way count: a program that leaves them out, or rounds other values in their place, can miss the bound.
Values may be sent and summed in bfloat16 or wider, within the bound.
A program may use at most 192 MiB of HBM per device.

```python
import math
import jax
import jax.numpy as jnp
from jax import lax

MODEL_DIMENSION = 1152
H = 16
HD = 72
FF = 4608
SLOTS = 1
STEP = 2
LATENT_TOKENS = 256
SLOT_COUNT = 16
LAT = 8
N_DP = 16


def slot_plan(key):
    key_owner = jax.random.fold_in(key, 11)
    key_order = jax.random.fold_in(key, 12)
    key_ids = jax.random.fold_in(key, 13)
    key_pad = jax.random.fold_in(key, 14)
    tickets = N_DP * SLOTS
    owner_group = jnp.arange(tickets, dtype=jnp.int32) // SLOTS
    chosen = jax.random.randint(key_owner, (), 0, N_DP, dtype=jnp.int32)
    shuffled = jax.random.permutation(key_order, tickets).astype(jnp.int32)
    ticket_score = jnp.where(owner_group == chosen, shuffled - tickets, shuffled)
    ticket_order = jnp.argsort(ticket_score, stable=True)
    taken_flags = jnp.zeros((tickets,), jnp.int32).at[ticket_order[:LAT]].set(1)
    counts = jnp.sum(taken_flags.reshape(N_DP, SLOTS), axis=1).astype(jnp.int32)
    live_flags = (jnp.arange(SLOTS, dtype=jnp.int32)[None, :] < counts[:, None]).reshape(-1)
    position = jnp.cumsum(live_flags.astype(jnp.int32)) - 1
    latent_perm = jax.random.permutation(key_ids, LAT).astype(jnp.int32)
    pad_ids = jax.random.randint(key_pad, (tickets,), 0, LAT, dtype=jnp.int32)
    latent_table = jnp.where(live_flags, latent_perm[jnp.clip(position, 0, LAT - 1)], pad_ids)
    return (counts, latent_table.reshape(N_DP, SLOTS).astype(jnp.int32))


def draw_slot_counts(key, part):
    return slot_plan(key)[0]


def draw_slot_latent(key, part):
    return slot_plan(key)[1]


def draw_qkv_weight(key, part):
    base_draw = jax.random.normal(key, (MODEL_DIMENSION, 3 * MODEL_DIMENSION), jnp.float32) * MODEL_DIMENSION ** (-0.5)
    base_draw = jnp.clip(base_draw, -6.0 * MODEL_DIMENSION ** (-0.5), 6.0 * MODEL_DIMENSION ** (-0.5))
    return base_draw


def level_of(stream_key, dims, cuts, smallest, top_value):
    def one(dim, blocks):
        heights = jax.random.uniform(jax.random.fold_in(jax.random.fold_in(stream_key, 6), dim), (blocks,), jnp.float32, smallest / len(cuts), top_value / len(cuts))
        return jnp.repeat(jnp.exp(heights), dims[dim] // blocks).reshape((-1,) + (1,) * (len(dims) - dim - 1))

    level = one(*cuts[0])
    for cut in cuts[1:]:
        level = level * one(*cut)
    return level


def bell_draw(own_key, shape, scale, most, shards=(), kind=jnp.bfloat16):
    values = jax.random.normal(own_key, shape, jnp.float32) * scale
    if len(shards) > 0:
        values = level_of(own_key, shape, shards, -0.22, 0.18) * values
    return jnp.clip(values, min=-most, max=most).astype(kind)


def setup_inputs(seed: int = 0) -> dict:
    arg_keys = jax.random.split(jax.random.key(seed), 36)
    latents = bell_draw(arg_keys[0], (SLOT_COUNT, LATENT_TOKENS, MODEL_DIMENSION), 1.0, 6.0, ((0, 16), (1, 2)), jnp.float32)
    condition = bell_draw(arg_keys[1], (LAT, MODEL_DIMENSION), 1.0, 6.0, (), jnp.float32)
    slot_latent = draw_slot_latent(jax.random.fold_in(arg_keys[35], 71), 0)
    slot_counts = draw_slot_counts(jax.random.fold_in(arg_keys[35], 71), 0)
    output_gradient = bell_draw(arg_keys[4], (SLOT_COUNT, LATENT_TOKENS, MODEL_DIMENSION), 1.0, 6.0, ((0, 16), (1, 2)), jnp.float32)
    ada_weight = bell_draw(arg_keys[5], (MODEL_DIMENSION, 6 * MODEL_DIMENSION), MODEL_DIMENSION ** -0.5, 0.1875, ((1, 32),), jnp.float32)
    ada_bias = bell_draw(arg_keys[6], (6 * MODEL_DIMENSION,), 0.3, 1.75, ((0, 32),), jnp.float32)
    qkv_weight = draw_qkv_weight(jax.random.fold_in(arg_keys[35], 71), 0)
    qkv_bias = bell_draw(arg_keys[8], (3 * MODEL_DIMENSION,), 0.2, 1.25, ((0, 2),), jnp.float32)
    out_weight = bell_draw(arg_keys[9], (MODEL_DIMENSION, MODEL_DIMENSION), (max(MODEL_DIMENSION // 16, 1)) ** -0.5, 0.75, ((0, 16), (1, 2)), jnp.float32)
    out_bias = bell_draw(arg_keys[10], (MODEL_DIMENSION,), 0.2, 1.25, ((0, 2),), jnp.float32)
    up_weight = bell_draw(arg_keys[11], (MODEL_DIMENSION, FF), MODEL_DIMENSION ** -0.5, 0.1875, ((0, 16), (1, 2)), jnp.float32)
    up_bias = bell_draw(arg_keys[12], (FF,), 0.2, 1.25, ((0, 2),), jnp.float32)
    down_weight = bell_draw(arg_keys[13], (FF, MODEL_DIMENSION), FF ** -0.5, 0.09375, ((0, 16), (1, 2)), jnp.float32)
    down_bias = bell_draw(arg_keys[14], (MODEL_DIMENSION,), 0.2, 1.25, ((0, 2),), jnp.float32)
    mean_adaw = bell_draw(arg_keys[15], (MODEL_DIMENSION, 6 * MODEL_DIMENSION), 3.0, 16.0, ((1, 32),), jnp.float32)
    mean_adab = bell_draw(arg_keys[16], (6 * MODEL_DIMENSION,), 3.0, 16.0, ((0, 32),), jnp.float32)
    mean_qkvw = bell_draw(arg_keys[17], (MODEL_DIMENSION, 3 * MODEL_DIMENSION), 3.0, 16.0, ((0, 16), (1, 2)), jnp.float32)
    mean_qkvb = bell_draw(arg_keys[18], (3 * MODEL_DIMENSION,), 3.0, 16.0, ((0, 2),), jnp.float32)
    mean_outw = bell_draw(arg_keys[19], (MODEL_DIMENSION, MODEL_DIMENSION), 3.0, 16.0, ((0, 16), (1, 2)), jnp.float32)
    mean_outb = bell_draw(arg_keys[20], (MODEL_DIMENSION,), 3.0, 16.0, ((0, 2),), jnp.float32)
    mean_upw = bell_draw(arg_keys[21], (MODEL_DIMENSION, FF), 3.0, 16.0, ((0, 16), (1, 2)), jnp.float32)
    mean_upb = bell_draw(arg_keys[22], (FF,), 3.0, 16.0, ((0, 2),), jnp.float32)
    mean_downw = bell_draw(arg_keys[23], (FF, MODEL_DIMENSION), 3.0, 16.0, ((0, 16), (1, 2)), jnp.float32)
    mean_downb = bell_draw(arg_keys[24], (MODEL_DIMENSION,), 3.0, 16.0, ((0, 2),), jnp.float32)
    sqmean_adaw = jnp.clip(jnp.exp(math.log(3.0) - 2.3025851 * jax.random.uniform(arg_keys[25], (MODEL_DIMENSION, 6 * MODEL_DIMENSION), jnp.float32) ** level_of(arg_keys[25], (MODEL_DIMENSION, 6 * MODEL_DIMENSION), ((1, 32),), -0.2, 0.2)), 0.3, 3.0)
    sqmean_adab = jnp.clip(jnp.exp(math.log(3.0) - 2.3025851 * jax.random.uniform(arg_keys[26], (6 * MODEL_DIMENSION,), jnp.float32) ** level_of(arg_keys[26], (6 * MODEL_DIMENSION,), ((0, 32),), -0.2, 0.2)), 0.3, 3.0)
    sqmean_qkvw = jnp.clip(jnp.exp(math.log(3.0) - 2.3025851 * jax.random.uniform(arg_keys[27], (MODEL_DIMENSION, 3 * MODEL_DIMENSION), jnp.float32) ** level_of(arg_keys[27], (MODEL_DIMENSION, 3 * MODEL_DIMENSION), ((0, 16), (1, 2)), -0.2, 0.2)), 0.3, 3.0)
    sqmean_qkvb = jnp.clip(jnp.exp(math.log(3.0) - 2.3025851 * jax.random.uniform(arg_keys[28], (3 * MODEL_DIMENSION,), jnp.float32) ** level_of(arg_keys[28], (3 * MODEL_DIMENSION,), ((0, 2),), -0.2, 0.2)), 0.3, 3.0)
    sqmean_outw = jnp.clip(jnp.exp(math.log(3.0) - 2.3025851 * jax.random.uniform(arg_keys[29], (MODEL_DIMENSION, MODEL_DIMENSION), jnp.float32) ** level_of(arg_keys[29], (MODEL_DIMENSION, MODEL_DIMENSION), ((0, 16), (1, 2)), -0.2, 0.2)), 0.3, 3.0)
    sqmean_outb = jnp.clip(jnp.exp(math.log(3.0) - 2.3025851 * jax.random.uniform(arg_keys[30], (MODEL_DIMENSION,), jnp.float32) ** level_of(arg_keys[30], (MODEL_DIMENSION,), ((0, 2),), -0.2, 0.2)), 0.3, 3.0)
    sqmean_upw = jnp.clip(jnp.exp(math.log(3.0) - 2.3025851 * jax.random.uniform(arg_keys[31], (MODEL_DIMENSION, FF), jnp.float32) ** level_of(arg_keys[31], (MODEL_DIMENSION, FF), ((0, 16), (1, 2)), -0.2, 0.2)), 0.3, 3.0)
    sqmean_upb = jnp.clip(jnp.exp(math.log(3.0) - 2.3025851 * jax.random.uniform(arg_keys[32], (FF,), jnp.float32) ** level_of(arg_keys[32], (FF,), ((0, 2),), -0.2, 0.2)), 0.3, 3.0)
    sqmean_downw = jnp.clip(jnp.exp(math.log(3.0) - 2.3025851 * jax.random.uniform(arg_keys[33], (FF, MODEL_DIMENSION), jnp.float32) ** level_of(arg_keys[33], (FF, MODEL_DIMENSION), ((0, 16), (1, 2)), -0.2, 0.2)), 0.3, 3.0)
    sqmean_downb = jnp.clip(jnp.exp(math.log(3.0) - 2.3025851 * jax.random.uniform(arg_keys[34], (MODEL_DIMENSION,), jnp.float32) ** level_of(arg_keys[34], (MODEL_DIMENSION,), ((0, 2),), -0.2, 0.2)), 0.3, 3.0)
    return {"latents": latents, "condition": condition, "slot_latent": slot_latent, "slot_counts": slot_counts, "output_gradient": output_gradient, "ada_weight": ada_weight, "ada_bias": ada_bias, "qkv_weight": qkv_weight, "qkv_bias": qkv_bias, "out_weight": out_weight, "out_bias": out_bias, "up_weight": up_weight, "up_bias": up_bias, "down_weight": down_weight, "down_bias": down_bias, "mean_adaw": mean_adaw, "mean_adab": mean_adab, "mean_qkvw": mean_qkvw, "mean_qkvb": mean_qkvb, "mean_outw": mean_outw, "mean_outb": mean_outb, "mean_upw": mean_upw, "mean_upb": mean_upb, "mean_downw": mean_downw, "mean_downb": mean_downb, "sqmean_adaw": sqmean_adaw, "sqmean_adab": sqmean_adab, "sqmean_qkvw": sqmean_qkvw, "sqmean_qkvb": sqmean_qkvb, "sqmean_outw": sqmean_outw, "sqmean_outb": sqmean_outb, "sqmean_upw": sqmean_upw, "sqmean_upb": sqmean_upb, "sqmean_downw": sqmean_downw, "sqmean_downb": sqmean_downb}


EPS_NORM = 1e-06
GELU_COEF = 0.7978845608
GELU_CUBE = 0.044715
BETA_ONE = 0.9
BETA_TWO = 0.999
LEARN_RATE = 0.05
EPS_ADAM = 1e-08

def rounded(values):
    return lax.optimization_barrier(values.astype(jnp.bfloat16)).astype(jnp.float32)

def normalize(values):
    center = values - lax.optimization_barrier(jnp.mean(values, axis=-1, keepdims=True))
    spread = lax.rsqrt(lax.optimization_barrier(jnp.mean(center * center, axis=-1, keepdims=True)) + EPS_NORM)
    return (center * spread, spread)

def norm_back(upstream, normed, spread):
    return spread * (upstream - lax.optimization_barrier(jnp.mean(upstream, axis=-1, keepdims=True)) - normed * lax.optimization_barrier(jnp.mean(upstream * normed, axis=-1, keepdims=True)))

def gelu_tanh(values):
    tanh_part = jnp.tanh(GELU_COEF * (values + GELU_CUBE * values * values * values))
    return 0.5 * values * (1.0 + tanh_part)

def gelu_slope(values):
    tanh_part = jnp.tanh(GELU_COEF * (values + GELU_CUBE * values * values * values))
    return 0.5 * (1.0 + tanh_part) + 0.5 * values * (1.0 - tanh_part * tanh_part) * GELU_COEF * (1.0 + 3.0 * GELU_CUBE * values * values)

def silu_slope(values):
    sigmoid_part = jax.nn.sigmoid(values)
    return sigmoid_part * (1.0 + values * (1.0 - sigmoid_part))

def adamw_step(parameter, gradient, first_mom, second):
    first_new = BETA_ONE * first_mom + (1.0 - BETA_ONE) * gradient
    second_new = BETA_TWO * second + (1.0 - BETA_TWO) * gradient * gradient
    first_hat = first_new / (1.0 - BETA_ONE ** STEP)
    second_hat = second_new / (1.0 - BETA_TWO ** STEP)
    return (parameter - LEARN_RATE * first_hat / (jnp.sqrt(second_hat) + EPS_ADAM), first_new, second_new)

def one_latent(tokens, upstream, modrow, params):
    mat_qkv, vec_qkv, mat_out, vec_out, mat_up, vec_up, mat_down, vec_down = params
    shift_att, scale_att, gate_att, shift_mlp, scale_mlp, gate_mlp = jnp.split(modrow, 6)
    seq_len = tokens.shape[0]
    scale = HD ** (-0.5)
    normed_att, spread_att = normalize(tokens)
    attn_in = (normed_att * (1.0 + scale_att) + shift_att).astype(jnp.bfloat16)
    qkv_all = rounded(jnp.dot(attn_in, mat_qkv, preferred_element_type=jnp.float32) + vec_qkv)
    queries = qkv_all[:, :MODEL_DIMENSION].reshape(seq_len, H, HD)
    keys_all = qkv_all[:, MODEL_DIMENSION:2 * MODEL_DIMENSION].reshape(seq_len, H, HD)
    values_all = qkv_all[:, 2 * MODEL_DIMENSION:].reshape(seq_len, H, HD)
    scores = jnp.einsum('qhd,khd->hqk', queries, keys_all) * scale
    row_max = lax.optimization_barrier(jnp.max(scores, axis=-1, keepdims=True))
    row_total = lax.optimization_barrier(jnp.sum(jnp.exp(scores - row_max), axis=-1, keepdims=True))
    attn_probs = jnp.exp(scores - row_max) / row_total
    probs_wide = rounded(attn_probs)
    attended = jnp.einsum('hqk,khd->qhd', probs_wide, values_all)
    attended_b = attended.reshape(seq_len, MODEL_DIMENSION).astype(jnp.bfloat16)
    branch_att = jnp.dot(attended_b, mat_out, preferred_element_type=jnp.float32) + vec_out
    middle = tokens + gate_att * branch_att
    normed_mlp, spread_mlp = normalize(middle)
    mlp_in = (normed_mlp * (1.0 + scale_mlp) + shift_mlp).astype(jnp.bfloat16)
    hidden = jnp.dot(mlp_in, mat_up, preferred_element_type=jnp.float32) + vec_up
    activated = gelu_tanh(hidden).astype(jnp.bfloat16)
    branch_mlp = jnp.dot(activated, mat_down, preferred_element_type=jnp.float32) + vec_down
    block_output = middle + gate_mlp * branch_mlp
    back_down = upstream * gate_mlp
    back_down_b = back_down.astype(jnp.bfloat16)
    grad_downw = jnp.dot(activated.T, back_down_b, preferred_element_type=jnp.float32)
    grad_downb = lax.optimization_barrier(jnp.sum(back_down, axis=0))
    back_hidden = jnp.dot(back_down_b, mat_down.T, preferred_element_type=jnp.float32) * gelu_slope(hidden)
    back_hidden_b = back_hidden.astype(jnp.bfloat16)
    grad_upw = jnp.dot(mlp_in.T, back_hidden_b, preferred_element_type=jnp.float32)
    grad_upb = lax.optimization_barrier(jnp.sum(back_hidden, axis=0))
    back_mlp_in = jnp.dot(back_hidden_b, mat_up.T, preferred_element_type=jnp.float32)
    back_middle = upstream + norm_back(back_mlp_in * (1.0 + scale_mlp), normed_mlp, spread_mlp)
    back_att = back_middle * gate_att
    back_att_b = back_att.astype(jnp.bfloat16)
    grad_outw = jnp.dot(attended_b.T, back_att_b, preferred_element_type=jnp.float32)
    grad_outb = lax.optimization_barrier(jnp.sum(back_att, axis=0))
    back_attended = rounded(jnp.dot(back_att_b, mat_out.T, preferred_element_type=jnp.float32)).reshape(seq_len, H, HD)
    back_probs = jnp.einsum('qhd,khd->hqk', back_attended, values_all)
    row_delta = jnp.einsum('qhd,qhd->hq', back_attended, attended)[:, :, None]
    back_scores = rounded(attn_probs * (back_probs - row_delta) * scale)
    back_queries = jnp.einsum('hqk,khd->qhd', back_scores, keys_all).reshape(seq_len, MODEL_DIMENSION)
    back_keys = jnp.einsum('hqk,qhd->khd', back_scores, queries).reshape(seq_len, MODEL_DIMENSION)
    back_values = jnp.einsum('hqk,qhd->khd', probs_wide, back_attended).reshape(seq_len, MODEL_DIMENSION)
    back_qkv = jnp.concatenate([back_queries, back_keys, back_values], axis=1)
    back_qkv_b = back_qkv.astype(jnp.bfloat16)
    grad_qkvw = jnp.dot(attn_in.T, back_qkv_b, preferred_element_type=jnp.float32)
    grad_qkvb = lax.optimization_barrier(jnp.sum(back_qkv, axis=0))
    back_attn_in = jnp.dot(back_qkv_b, mat_qkv.T, preferred_element_type=jnp.float32)
    back_tokens = back_middle + norm_back(back_attn_in * (1.0 + scale_att), normed_att, spread_att)
    modgrad = jnp.concatenate([lax.optimization_barrier(jnp.sum(back_attn_in, axis=0)), lax.optimization_barrier(jnp.sum(back_attn_in * normed_att, axis=0)), lax.optimization_barrier(jnp.sum(back_middle * branch_att, axis=0)), lax.optimization_barrier(jnp.sum(back_mlp_in, axis=0)), lax.optimization_barrier(jnp.sum(back_mlp_in * normed_mlp, axis=0)), lax.optimization_barrier(jnp.sum(upstream * branch_mlp, axis=0))])
    gradients = (grad_qkvw, grad_qkvb, grad_outw, grad_outb, grad_upw, grad_upb, grad_downw, grad_downb)
    return (block_output, back_tokens, modgrad, gradients)

def reference(latents, condition, slot_latent, slot_counts, output_gradient, ada_weight, ada_bias, qkv_weight, qkv_bias, out_weight, out_bias, up_weight, up_bias, down_weight, down_bias, mean_adaw, mean_adab, mean_qkvw, mean_qkvb, mean_outw, mean_outb, mean_upw, mean_upb, mean_downw, mean_downb, sqmean_adaw, sqmean_adab, sqmean_qkvw, sqmean_qkvb, sqmean_outw, sqmean_outb, sqmean_upw, sqmean_upb, sqmean_downw, sqmean_downb):
    live_slots = (jnp.arange(SLOTS)[None, :] < slot_counts[:, None]).reshape(-1)
    latent_ids = slot_latent.reshape(-1)
    slot_matches = (latent_ids[:, None] == jnp.arange(LAT)[None, :]) & live_slots[:, None]
    slot_lookup = lax.optimization_barrier(jnp.sum(jnp.where(slot_matches, jnp.arange(SLOT_COUNT)[:, None], 0), axis=0)).astype(jnp.int32)
    silu_cond = jax.nn.silu(condition).astype(jnp.bfloat16)
    modulation = jnp.dot(silu_cond, ada_weight.astype(jnp.bfloat16), preferred_element_type=jnp.float32) + rounded(ada_bias)
    params = (qkv_weight.astype(jnp.bfloat16), rounded(qkv_bias), out_weight.astype(jnp.bfloat16), rounded(out_bias), up_weight.astype(jnp.bfloat16), rounded(up_bias), down_weight.astype(jnp.bfloat16), rounded(down_bias))
    starting = tuple((jnp.zeros(item.shape, jnp.float32) for item in (qkv_weight, qkv_bias, out_weight, out_bias, up_weight, up_bias, down_weight, down_bias)))

    def scan_step(totals, latent_index):
        slot_index = slot_lookup[latent_index]
        tokens = lax.dynamic_index_in_dim(latents, slot_index, 0, keepdims=False)
        upstream = lax.dynamic_index_in_dim(output_gradient, slot_index, 0, keepdims=False)
        block_output, back_tokens, modgrad, gradients = one_latent(tokens, upstream, modulation[latent_index], params)
        totals = jax.tree.map(jnp.add, totals, gradients)
        return (totals, (block_output, back_tokens, modgrad))
    totals, (forward_results, backward_results, modgrads) = lax.scan(scan_step, starting, jnp.arange(LAT))
    block_output = jnp.zeros((SLOT_COUNT, LATENT_TOKENS, MODEL_DIMENSION), jnp.float32).at[slot_lookup].set(forward_results)
    latent_gradient = jnp.zeros((SLOT_COUNT, LATENT_TOKENS, MODEL_DIMENSION), jnp.float32).at[slot_lookup].set(backward_results)
    grad_adaw = jnp.dot(rounded(jax.nn.silu(condition)).T, modgrads, precision=lax.Precision.HIGHEST)
    grad_adab = lax.optimization_barrier(jnp.sum(modgrads, axis=0))
    condition_grad = jnp.dot(modgrads, rounded(ada_weight).T, precision=lax.Precision.HIGHEST) * silu_slope(condition)
    grads_all = (grad_adaw, grad_adab) + tuple(totals)
    params_all = (ada_weight, ada_bias, qkv_weight, qkv_bias, out_weight, out_bias, up_weight, up_bias, down_weight, down_bias)
    means_all = (mean_adaw, mean_adab, mean_qkvw, mean_qkvb, mean_outw, mean_outb, mean_upw, mean_upb, mean_downw, mean_downb)
    squares_all = (sqmean_adaw, sqmean_adab, sqmean_qkvw, sqmean_qkvb, sqmean_outw, sqmean_outb, sqmean_upw, sqmean_upb, sqmean_downw, sqmean_downb)
    updates = [adamw_step(p_item, g_item, m_item, v_item) for p_item, g_item, m_item, v_item in zip(params_all, grads_all, means_all, squares_all)]
    newvals = tuple((entry[0] for entry in updates))
    newmeans = tuple((entry[1] for entry in updates))
    newsqrs = tuple((entry[2] for entry in updates))
    return (block_output, latent_gradient, condition_grad) + grads_all + newvals + newmeans + newsqrs
```

```python
import jax
import jax.numpy as jnp
from jax import lax
from jax.sharding import PartitionSpec as P

H = 16
HD = 72
STEP = 2


EPS_NORM = 1e-06
GELU_COEF = 0.7978845608
GELU_CUBE = 0.044715
BETA_ONE = 0.9
BETA_TWO = 0.999
LEARN_RATE = 0.05
EPS_ADAM = 1e-08


def rounded(values):
    return lax.optimization_barrier(values.astype(jnp.bfloat16)).astype(jnp.float32)


def normalize(values):
    center = values - jnp.mean(values, axis=-1, keepdims=True)
    spread = lax.rsqrt(jnp.mean(center * center, axis=-1, keepdims=True) + EPS_NORM)
    return (center * spread, spread)


def norm_back(upstream, normed, spread):
    return spread * (
        upstream
        - jnp.mean(upstream, axis=-1, keepdims=True)
        - normed * jnp.mean(upstream * normed, axis=-1, keepdims=True)
    )


def gelu_tanh(values):
    tanh_part = jnp.tanh(GELU_COEF * (values + GELU_CUBE * values * values * values))
    return 0.5 * values * (1.0 + tanh_part)


def gelu_slope(values):
    tanh_part = jnp.tanh(GELU_COEF * (values + GELU_CUBE * values * values * values))
    return 0.5 * (1.0 + tanh_part) + 0.5 * values * (1.0 - tanh_part * tanh_part) * GELU_COEF * (
        1.0 + 3.0 * GELU_CUBE * values * values
    )


def silu_slope(values):
    sigmoid_part = jax.nn.sigmoid(values)
    return sigmoid_part * (1.0 + values * (1.0 - sigmoid_part))


def adamw_step(parameter, gradient, first_mom, second):
    first_new = BETA_ONE * first_mom + (1.0 - BETA_ONE) * gradient
    second_new = BETA_TWO * second + (1.0 - BETA_TWO) * gradient * gradient
    first_hat = first_new / (1.0 - BETA_ONE**STEP)
    second_hat = second_new / (1.0 - BETA_TWO**STEP)
    return (
        parameter - LEARN_RATE * first_hat / (jnp.sqrt(second_hat) + EPS_ADAM),
        first_new,
        second_new,
    )


def flat_index(axes):
    index = lax.axis_index(axes[0])
    for axis in axes[1:]:
        index = index * lax.axis_size(axis) + lax.axis_index(axis)
    return index


def swap_bit(values, axes, step):
    total = 1
    for axis in axes:
        total *= lax.axis_size(axis)
    return lax.ppermute(values, axes, [(i, i ^ step) for i in range(total)])


def axes_size(axes):
    total = 1
    for axis in axes:
        total *= lax.axis_size(axis)
    return total


def gather_tree(values, axes):
    index, blocks, step = flat_index(axes), values[None], 1
    while step < axes_size(axes):
        other = swap_bit(blocks, axes, step)
        upper = (index // step) % 2 == 1
        blocks = jnp.concatenate(
            [jnp.where(upper, other, blocks), jnp.where(upper, blocks, other)], axis=0
        )
        step *= 2
    return blocks


def scatter_tree(blocks, axes, sent=None):
    index, step = flat_index(axes), axes_size(axes) // 2
    while step >= 1:
        low, high = blocks[:step], blocks[step:]
        upper = (index // step) % 2 == 1
        away = jnp.where(upper, low, high)
        if sent is not None:
            away = away.astype(sent)
        kept = jnp.where(upper, high, low)
        blocks = kept + swap_bit(away, axes, step).astype(kept.dtype)
        step //= 2
    return blocks[0]


def sum_tree(values, axes):
    step = 1
    while step < axes_size(axes):
        values = values + swap_bit(values, axes, step)
        step *= 2
    return values


def join_columns(halves, widths):
    parts, start = [], 0
    for width in widths:
        part = halves[:, :, start : start + width]
        parts.append(jnp.moveaxis(part, 0, 1).reshape(part.shape[1], -1))
        start += width
    return parts


def split_columns(parts):
    ways = lax.axis_size("seq")
    blocks = [
        jnp.moveaxis(part.reshape(part.shape[0], ways, -1), 1, 0) for part in parts
    ]
    return jnp.concatenate(blocks, axis=2)


def weight_term(left, right):
    return jnp.einsum("rc,rd->cd", left, right, preferred_element_type=jnp.float32).astype(
        jnp.bfloat16
    )


def spread_terms(terms):
    widths = [term.shape[1] // lax.axis_size("seq") for term in terms]
    joined = jnp.concatenate(terms, axis=1) if len(terms) > 1 else terms[0]
    rows = lax.psum_scatter(joined, "dp", scatter_dimension=0, tiled=True)
    pieces, start = [], 0
    for term in terms:
        pieces.append(rows[:, start : start + term.shape[1]])
        start += term.shape[1]
    own = scatter_tree(split_columns(pieces).astype(jnp.float32), ("seq",), jnp.bfloat16)
    blocks, start = [], 0
    for width in widths:
        blocks.append(own[:, start : start + width])
        start += width
    return blocks


def on_device(
    latents,
    condition,
    slot_latent,
    slot_counts,
    output_gradient,
    ada_weight,
    ada_bias,
    qkv_weight,
    qkv_bias,
    out_weight,
    out_bias,
    up_weight,
    up_bias,
    down_weight,
    down_bias,
    mean_adaw,
    mean_adab,
    mean_qkvw,
    mean_qkvb,
    mean_outw,
    mean_outb,
    mean_upw,
    mean_upb,
    mean_downw,
    mean_downb,
    sqmean_adaw,
    sqmean_adab,
    sqmean_qkvw,
    sqmean_qkvb,
    sqmean_outw,
    sqmean_outb,
    sqmean_upw,
    sqmean_upb,
    sqmean_downw,
    sqmean_downb,
):
    slot_total, tok_dev, model_width = latents.shape
    row_count = slot_total * tok_dev
    scale = HD ** (-0.5)
    live_slots = jnp.arange(slot_total) < slot_counts[0]
    live_mask = live_slots[:, None, None]
    latent_count = condition.shape[0]
    slot_matches = (
        (slot_latent[0][:, None] == jnp.arange(latent_count)[None, :]) & live_slots[:, None]
    ).astype(jnp.float32)
    silu_cond = jax.nn.silu(condition).astype(jnp.bfloat16)
    mod_cols = jnp.dot(
        silu_cond, ada_weight.astype(jnp.bfloat16), preferred_element_type=jnp.float32
    ) + rounded(ada_bias)
    modulation = jnp.moveaxis(gather_tree(mod_cols, ("dp", "seq")), 0, 1).reshape(
        latent_count, -1
    )
    slot_mod = jnp.dot(slot_matches, modulation, precision=lax.Precision.HIGHEST)[:, None, :]
    shift_att, scale_att, gate_att, shift_mlp, scale_mlp, gate_mlp = jnp.split(slot_mod, 6, axis=2)
    upstream = jnp.where(live_mask, output_gradient, 0.0)
    biases = (qkv_bias, out_bias, up_bias, down_bias)
    bias_rows = gather_tree(
        jnp.concatenate(biases).astype(jnp.bfloat16)[None], ("seq",)
    )
    vec_qkv, vec_out, vec_up, vec_down = (
        part[0].astype(jnp.float32)
        for part in join_columns(bias_rows, [item.shape[0] for item in biases])
    )
    wide = (qkv_weight, out_weight, up_weight)
    wide_halves = gather_tree(jnp.concatenate(wide, axis=1).astype(jnp.bfloat16), ("seq",))
    wide_rows = jnp.concatenate(
        join_columns(wide_halves, [item.shape[1] for item in wide]), axis=1
    )
    wide_full = lax.all_gather(wide_rows, "dp", axis=0, tiled=True)
    qkv_end = 3 * model_width
    mat_qkv = wide_full[:, :qkv_end]
    mat_out = wide_full[:, qkv_end : qkv_end + model_width]
    mat_up = wide_full[:, qkv_end + model_width :]
    down_halves = gather_tree(down_weight.astype(jnp.bfloat16), ("seq",))
    down_rows = join_columns(down_halves, [down_weight.shape[1]])[0]
    mat_down = lax.all_gather(down_rows, "dp", axis=0, tiled=True)
    normed_att, spread_att = normalize(latents)
    attn_in = (
        (normed_att * (1.0 + scale_att) + shift_att)
        .astype(jnp.bfloat16)
        .reshape(row_count, model_width)
    )
    qkv_all = (jnp.dot(attn_in, mat_qkv, preferred_element_type=jnp.float32) + vec_qkv).astype(
        jnp.bfloat16
    )
    queries = qkv_all[:, :model_width].reshape(slot_total, tok_dev, H, HD)
    keys_own = qkv_all[:, model_width : 2 * model_width].reshape(slot_total, tok_dev, model_width)
    values_own = qkv_all[:, 2 * model_width :].reshape(slot_total, tok_dev, model_width)
    pairs_own = jnp.concatenate([keys_own, values_own], axis=2)
    pairs_all = jnp.moveaxis(gather_tree(pairs_own, ("seq",)), 0, 1)
    pairs_all = pairs_all.reshape(slot_total, -1, 2 * model_width)
    keys_all, values_all = pairs_all[:, :, :model_width], pairs_all[:, :, model_width:]
    keys_heads = keys_all.reshape(slot_total, -1, H, HD)
    values_heads = values_all.reshape(slot_total, -1, H, HD)
    scores = (
        jnp.einsum("sqhd,skhd->shqk", queries, keys_heads, preferred_element_type=jnp.float32)
        * scale
    )
    row_max = jnp.max(scores, axis=-1, keepdims=True)
    row_total = jnp.sum(jnp.exp(scores - row_max), axis=-1, keepdims=True)
    attn_probs = jnp.exp(scores - row_max) / row_total
    probs_b = attn_probs.astype(jnp.bfloat16)
    attended = jnp.einsum(
        "shqk,skhd->sqhd", probs_b, values_heads, preferred_element_type=jnp.float32
    )
    attended_b = attended.reshape(row_count, model_width).astype(jnp.bfloat16)
    branch_att = (
        jnp.dot(attended_b, mat_out, preferred_element_type=jnp.float32) + vec_out
    ).reshape(slot_total, tok_dev, model_width)
    middle = latents + gate_att * branch_att
    normed_mlp, spread_mlp = normalize(middle)
    mlp_in = (
        (normed_mlp * (1.0 + scale_mlp) + shift_mlp)
        .astype(jnp.bfloat16)
        .reshape(row_count, model_width)
    )
    hidden = jnp.dot(mlp_in, mat_up, preferred_element_type=jnp.float32) + vec_up
    activated = gelu_tanh(hidden).astype(jnp.bfloat16)
    activated, mat_down = lax.optimization_barrier((activated, mat_down))
    branch_mlp = (
        jnp.dot(activated, mat_down, preferred_element_type=jnp.float32) + vec_down
    ).reshape(slot_total, tok_dev, model_width)
    block_output = jnp.where(live_mask, middle + gate_mlp * branch_mlp, 0.0)
    back_down = upstream * gate_mlp
    back_down_b = back_down.astype(jnp.bfloat16).reshape(row_count, model_width)
    (grad_downw,) = spread_terms([weight_term(activated, back_down_b)])
    sum_downb = jnp.sum(back_down, axis=(0, 1))
    back_hidden = jnp.einsum(
        "rd,fd->rf", back_down_b, mat_down, preferred_element_type=jnp.float32
    ) * gelu_slope(hidden)
    back_hidden_b = back_hidden.astype(jnp.bfloat16)
    term_up = weight_term(mlp_in, back_hidden_b)
    sum_upb = jnp.sum(back_hidden, axis=0)
    back_mlp_in = jnp.einsum(
        "rf,cf->rc", back_hidden_b, mat_up, preferred_element_type=jnp.float32
    ).reshape(slot_total, tok_dev, model_width)
    back_middle = upstream + norm_back(back_mlp_in * (1.0 + scale_mlp), normed_mlp, spread_mlp)
    back_att = back_middle * gate_att
    back_att_b = back_att.astype(jnp.bfloat16).reshape(row_count, model_width)
    term_out = weight_term(attended_b, back_att_b)
    sum_outb = jnp.sum(back_att, axis=(0, 1))
    back_attended = jnp.einsum(
        "rd,cd->rc", back_att_b, mat_out, preferred_element_type=jnp.float32
    ).astype(jnp.bfloat16)
    back_attended = back_attended.reshape(slot_total, tok_dev, H, HD)
    back_probs = jnp.einsum(
        "sqhd,skhd->shqk", back_attended, values_heads, preferred_element_type=jnp.float32
    )
    row_delta = jnp.einsum("sqhd,sqhd->shq", back_attended.astype(jnp.float32), attended)[..., None]
    back_scores = (attn_probs * (back_probs - row_delta) * scale).astype(jnp.bfloat16)
    back_queries = jnp.einsum(
        "shqk,skhd->sqhd", back_scores, keys_heads, preferred_element_type=jnp.float32
    )
    key_terms = jnp.einsum(
        "shqk,sqhd->skhd", back_scores, queries, preferred_element_type=jnp.float32
    ).reshape(slot_total, -1, model_width)
    value_terms = jnp.einsum(
        "shqk,sqhd->skhd", probs_b, back_attended, preferred_element_type=jnp.float32
    ).reshape(slot_total, -1, model_width)
    pair_terms = jnp.concatenate([key_terms, value_terms], axis=2)
    pair_terms = pair_terms.reshape(slot_total, -1, tok_dev, 2 * model_width)
    back_pairs = scatter_tree(jnp.moveaxis(pair_terms, 1, 0), ("seq",), jnp.bfloat16)
    back_keys, back_values = back_pairs[:, :, :model_width], back_pairs[:, :, model_width:]
    back_qkv = jnp.concatenate(
        [
            back_queries.reshape(row_count, model_width),
            back_keys.reshape(row_count, model_width),
            back_values.reshape(row_count, model_width),
        ],
        axis=1,
    )
    back_qkv_b = back_qkv.astype(jnp.bfloat16)
    term_qkv = weight_term(attn_in, back_qkv_b)
    grad_qkvw, grad_outw, grad_upw = spread_terms([term_qkv, term_out, term_up])
    sum_qkvb = jnp.sum(back_qkv, axis=0)
    back_attn_in = jnp.einsum(
        "rd,cd->rc", back_qkv_b, mat_qkv, preferred_element_type=jnp.float32
    ).reshape(slot_total, tok_dev, model_width)
    latent_gradient = jnp.where(
        live_mask,
        back_middle + norm_back(back_attn_in * (1.0 + scale_att), normed_att, spread_att),
        0.0,
    )
    slot_modgrad = jnp.concatenate(
        [
            jnp.sum(back_attn_in, axis=1),
            jnp.sum(back_attn_in * normed_att, axis=1),
            jnp.sum(back_middle * branch_att, axis=1),
            jnp.sum(back_mlp_in, axis=1),
            jnp.sum(back_mlp_in * normed_mlp, axis=1),
            jnp.sum(upstream * branch_mlp, axis=1),
        ],
        axis=1,
    )
    modgrad_table = jnp.dot(slot_matches.T, slot_modgrad, precision=lax.Precision.HIGHEST)
    modgrad_cols = scatter_tree(
        jnp.moveaxis(modgrad_table.reshape(latent_count, -1, ada_bias.shape[0]), 1, 0),
        ("dp", "seq"),
    )
    grad_adaw = jnp.dot(
        rounded(jax.nn.silu(condition)).T, modgrad_cols, precision=lax.Precision.HIGHEST
    )
    grad_adab = jnp.sum(modgrad_cols, axis=0)
    cond_term = jnp.dot(modgrad_cols, rounded(ada_weight).T, precision=lax.Precision.HIGHEST)
    cond_sum = sum_tree(cond_term, ("dp", "seq"))
    bias_sums = (sum_qkvb, sum_outb, sum_upb, sum_downb)
    totals, start, bias_totals = sum_tree(jnp.concatenate(bias_sums), ("dp", "seq")), 0, []
    for item in bias_sums:
        bias_totals.append(totals[start : start + item.shape[0]])
        start += item.shape[0]
    total_qkvb, total_outb, total_upb, total_downb = bias_totals
    condition_grad = cond_sum * silu_slope(condition)
    seq_index = lax.axis_index("seq")

    def own_part(full_sum, local_bias):
        length = local_bias.shape[0]
        return lax.dynamic_slice_in_dim(full_sum, seq_index * length, length)

    grad_qkvb = own_part(total_qkvb, qkv_bias)
    grad_outb = own_part(total_outb, out_bias)
    grad_upb = own_part(total_upb, up_bias)
    grad_downb = own_part(total_downb, down_bias)
    grads_all = (
        grad_adaw,
        grad_adab,
        grad_qkvw,
        grad_qkvb,
        grad_outw,
        grad_outb,
        grad_upw,
        grad_upb,
        grad_downw,
        grad_downb,
    )
    params_all = (
        ada_weight,
        ada_bias,
        qkv_weight,
        qkv_bias,
        out_weight,
        out_bias,
        up_weight,
        up_bias,
        down_weight,
        down_bias,
    )
    means_all = (
        mean_adaw,
        mean_adab,
        mean_qkvw,
        mean_qkvb,
        mean_outw,
        mean_outb,
        mean_upw,
        mean_upb,
        mean_downw,
        mean_downb,
    )
    squares_all = (
        sqmean_adaw,
        sqmean_adab,
        sqmean_qkvw,
        sqmean_qkvb,
        sqmean_outw,
        sqmean_outb,
        sqmean_upw,
        sqmean_upb,
        sqmean_downw,
        sqmean_downb,
    )
    updates = [
        adamw_step(p_item, g_item, m_item, v_item)
        for p_item, g_item, m_item, v_item in zip(params_all, grads_all, means_all, squares_all)
    ]
    newvals = tuple((entry[0] for entry in updates))
    newmeans = tuple((entry[1] for entry in updates))
    newsqrs = tuple((entry[2] for entry in updates))
    return (
        (block_output, latent_gradient, condition_grad) + grads_all + newvals + newmeans + newsqrs
    )


def solution(mesh):
    return jax.shard_map(
        on_device,
        mesh=mesh,
        in_specs=(
            P("dp", "seq", None),
            P(),
            P("dp", None),
            P("dp"),
            P("dp", "seq", None),
            P(None, ("dp", "seq")),
            P(("dp", "seq")),
            P("dp", "seq"),
            P("seq"),
            P("dp", "seq"),
            P("seq"),
            P("dp", "seq"),
            P("seq"),
            P("dp", "seq"),
            P("seq"),
            P(None, ("dp", "seq")),
            P(("dp", "seq")),
            P("dp", "seq"),
            P("seq"),
            P("dp", "seq"),
            P("seq"),
            P("dp", "seq"),
            P("seq"),
            P("dp", "seq"),
            P("seq"),
            P(None, ("dp", "seq")),
            P(("dp", "seq")),
            P("dp", "seq"),
            P("seq"),
            P("dp", "seq"),
            P("seq"),
            P("dp", "seq"),
            P("seq"),
            P("dp", "seq"),
            P("seq"),
        ),
        out_specs=(
            P("dp", "seq", None),
            P("dp", "seq", None),
            P(),
            P(None, ("dp", "seq")),
            P(("dp", "seq")),
            P("dp", "seq"),
            P("seq"),
            P("dp", "seq"),
            P("seq"),
            P("dp", "seq"),
            P("seq"),
            P("dp", "seq"),
            P("seq"),
            P(None, ("dp", "seq")),
            P(("dp", "seq")),
            P("dp", "seq"),
            P("seq"),
            P("dp", "seq"),
            P("seq"),
            P("dp", "seq"),
            P("seq"),
            P("dp", "seq"),
            P("seq"),
            P(None, ("dp", "seq")),
            P(("dp", "seq")),
            P("dp", "seq"),
            P("seq"),
            P("dp", "seq"),
            P("seq"),
            P("dp", "seq"),
            P("seq"),
            P("dp", "seq"),
            P("seq"),
            P(None, ("dp", "seq")),
            P(("dp", "seq")),
            P("dp", "seq"),
            P("seq"),
            P("dp", "seq"),
            P("seq"),
            P("dp", "seq"),
            P("seq"),
            P("dp", "seq"),
            P("seq"),
        ),
        check_vma=False,
    )
```
